128 devices in a mesh: pairs: 4 (over y_hi, core), stripe: 32 (over z, y_lo, x).
Axes of the slice: x: 4, y: 4 (y_hi: 2, y_lo: 2; y = y_hi * 2 + y_lo), z: 4, core: 2. Of those that a mesh axis runs over, the one named last changes fastest.
Arguments:
- slc_stack: bfloat16 [256, 2, 128, 4096], P(('pairs', 'stripe')), may hold values from -16 to 16
- az_offset: int32 [256], replicated, may hold values from -8 to 8
- rg_offset: int32 [256], replicated, may hold values from -16 to 16
- pair_list: int32 [1000, 2], replicated, may hold values from 0 to 255, as said below
Outputs:
- screen: float32 [256, 2, 32, 256], P(None, None, 'pairs', 'stripe')
- motion: float32 [256, 2, 32, 256], P(None, None, 'pairs', 'stripe')
The draws below stay inside these ranges and needn't reach their ends.
Inputs may be any that keep to these rules, and one draw needn't show every extreme that they name: `pair_list`: rows g * 250 to (g + 1) * 250 - 1 form pair group g: their reference dates lie in g * 64 to (g + 1) * 64 - 1, each secondary date is 1 to 5 dates after its reference, and no pair repeats.
All inputs are finite; a program needn't handle non-finite values.
Results may differ from the reference program's by a relative error of at most 0.0029.
Values may be sent and summed in bfloat16 or wider, within the bound.
A program may use at most 64 MiB of HBM per device.

```python
import jax
import jax.numpy as jnp
from jax import lax

DATES = 256
DATE_BLK = 64
PAIR_GRP = 250
PAIRS = 1000
MAXB = 5
LA = 4
LR = 16
MAXA = 8
MAXR = 16
FILTER_R = 3
AZ = 128
RANGE = 4096
MLR = 32
MLC = 256


def draw_pair_list(key, part):
    group_total = PAIRS // PAIR_GRP
    combos = DATE_BLK * MAXB
    combo_ids = jnp.arange(combos, dtype=jnp.int32)
    ref_offsets = combo_ids // MAXB
    date_gaps = combo_ids % MAXB + 1

    def draw_group(group_key, group_index):
        ref_dates = group_index * DATE_BLK + ref_offsets
        sec_dates = ref_dates + date_gaps
        scores = jax.random.permutation(group_key, combos).astype(jnp.int32)
        forced = (ref_offsets == DATE_BLK - 1) & (date_gaps == MAXB)
        scores = jnp.where(forced, -1, scores)
        scores = jnp.where(sec_dates <= DATES - 1, scores, combos + combo_ids)
        chosen = jnp.argsort(scores, stable=True)[:PAIR_GRP]
        return jnp.stack([ref_dates[chosen], sec_dates[chosen]], axis=1)
    group_keys = jax.random.split(jax.random.fold_in(key, 17), group_total)
    drawn = jax.vmap(draw_group)(group_keys, jnp.arange(group_total, dtype=jnp.int32))
    return drawn.reshape(PAIRS, 2).astype(jnp.int32)


def with_ends(result, rng, least, high):
    longest = result.shape.index(max(result.shape))
    spots = []
    for shift in (0, 1):
        where = [jax.random.randint(jax.random.fold_in(rng, axis), (), 0, length) for axis, length in enumerate(result.shape)]
        where[longest] = (where[longest] + shift) % result.shape[longest]
        spots.append(tuple(where))
    return result.at[spots[0]].set(least).at[spots[1]].set(high)


def steps_of(key, shape, shards, smallest, high):
    def one(dim, parts):
        heights = jax.random.uniform(jax.random.fold_in(jax.random.fold_in(key, 6), dim), (parts,), jnp.float32, smallest / len(shards), high / len(shards))
        return jnp.repeat(jnp.exp(heights), shape[dim] // parts).reshape((-1,) + (1,) * (len(shape) - dim - 1))

    level = one(*shards[0])
    for cut in shards[1:]:
        level = level * one(*cut)
    return level


def bell_draw(own_key, shape, spread, most, pieces=(), kind=jnp.bfloat16):
    array = spread * jax.random.normal(own_key, shape, jnp.float32)
    if pieces:
        array = array * steps_of(own_key, shape, pieces, -0.22, 0.18)
    return jnp.clip(array, -most, most).astype(kind)


def setup_inputs(seed: int = 0) -> dict:
    key_of = jax.random.split(jax.random.key(seed), 5)
    slc_stack = bell_draw(key_of[0], (DATES, 2, AZ, RANGE), 3.0, 16.0, ((0, 128),))
    az_offset = with_ends(jax.random.randint(key_of[1], (DATES,), 0 - MAXA, MAXA + 1), jax.random.fold_in(key_of[1], 1), 0 - MAXA, MAXA).astype(jnp.int32)
    rg_offset = with_ends(jax.random.randint(key_of[2], (DATES,), 0 - MAXR, MAXR + 1), jax.random.fold_in(key_of[2], 1), 0 - MAXR, MAXR).astype(jnp.int32)
    pair_list = draw_pair_list(jax.random.fold_in(key_of[4], 71), 0)
    return {"slc_stack": slc_stack, "az_offset": az_offset, "rg_offset": rg_offset, "pair_list": pair_list}


damping = 0.5

def resample(picture, az_shift, rg_shift):
    padded = jnp.pad(picture, ((0, 0), (MAXA, MAXA), (MAXR, MAXR)))
    starts = (jnp.int32(0), (az_shift + MAXA).astype(jnp.int32), (rg_shift + MAXR).astype(jnp.int32))
    return lax.dynamic_slice(padded, starts, (2, AZ, RANGE))

def form_pair(slc_stack, az_offset, rg_offset, pair_row):
    ref_date = pair_row[0]
    sec_date = pair_row[1]
    ref_image = resample(slc_stack[ref_date], az_offset[ref_date], rg_offset[ref_date]).astype(jnp.float32)
    sec_image = resample(slc_stack[sec_date], az_offset[sec_date], rg_offset[sec_date]).astype(jnp.float32)
    real_part = ref_image[0] * sec_image[0] + ref_image[1] * sec_image[1]
    imag_part = ref_image[1] * sec_image[0] - ref_image[0] * sec_image[1]
    product = jnp.stack([real_part, imag_part])
    summed = product.reshape(2, AZ // LA, LA, RANGE // LR, LR).sum(axis=(2, 4))
    return (summed / (LA * LR)).astype(jnp.bfloat16)

def filter_weights(extent):
    positions = jnp.arange(extent, dtype=jnp.int32)
    offsets = (positions[None, :] - positions[:, None]).astype(jnp.float32)
    sigma = FILTER_R / 2.0
    tap_weights = jnp.where(jnp.abs(offsets) <= FILTER_R, jnp.exp(-(offsets * offsets) / (2.0 * sigma * sigma)), 0.0)
    return tap_weights / jnp.sum(tap_weights, axis=1, keepdims=True)

def reference(slc_stack, az_offset, rg_offset, pair_list):
    multilooked = lax.map(lambda pair_row: form_pair(slc_stack, az_offset, rg_offset, pair_row), pair_list)
    date_ids = jnp.arange(DATES, dtype=jnp.int32)
    design = (pair_list[:, 0:1] == date_ids[None, :]).astype(jnp.float32) - (pair_list[:, 1:2] == date_ids[None, :]).astype(jnp.float32)
    highest = lax.Precision.HIGHEST
    normal = jnp.dot(design.T, design, precision=highest) + damping * jnp.eye(DATES, dtype=jnp.float32)
    right = jnp.dot(design.T, multilooked.reshape(PAIRS, -1).astype(jnp.float32), precision=highest)
    series = jnp.linalg.solve(normal, right).reshape(DATES, 2, MLR, MLC)
    row_filter = filter_weights(MLR)
    col_filter = filter_weights(MLC)
    screen = jnp.einsum('uw,dcwv->dcuv', row_filter, series, precision=highest)
    screen = jnp.einsum('dcuw,vw->dcuv', screen, col_filter, precision=highest)
    return (screen, series - screen)
```

```python
import math

import jax
import jax.numpy as jnp
from jax import lax
from jax.experimental import pallas as pl
from jax.experimental.pallas import tpu as pltpu
from jax.sharding import PartitionSpec as P

MESH = pl.DeviceIdType.MESH
HIGHEST = lax.Precision.HIGHEST
F32 = jnp.float32
BF16 = jnp.bfloat16

GROUPS = 4
STRIPES = 32
DATES = 256
BLOCK = 64
GAPS = 5
COMBOS = BLOCK * GAPS
AHEAD = 3
LINES = 128
CHUNK = LINES // GROUPS
WIDTH = 128
RANGE = STRIPES * WIDTH
TILE = 128
MROWS = 8
ROWS = 72
LIST = 1024
RADIUS = 3
DAMPING = 0.5
NEWTON = 9
START = 2.0 / 21.0
SPREAD = 2.0 * (RADIUS / 2.0) ** 2


def iota(shape, dim):
    return lax.broadcasted_iota(jnp.int32, shape, dim)


def dot(a, b, precision=None):
    return lax.dot_general(
        a, b, (((1,), (0,)), ((), ())), precision=precision, preferred_element_type=F32
    )


def dot_lanes(a, b):
    return lax.dot_general(a, b, (((1,), (1,)), ((), ())), preferred_element_type=F32)


def offset_of(k):
    n = lax.rem(k + 1, 4)
    dx = n + n // 2 - 2 * (n // 3)
    dy = 1 - lax.rem(k, 8) // 4
    dz = lax.rem(dx + k // 8, 4)
    return dz, dy, dx


SELF = 7


def edge_weight(position, whole):
    total = jnp.zeros(position.shape, F32)
    for k in range(-RADIUS, RADIUS + 1):
        inside = (position + k >= 0) & (position + k < whole)
        total = total + jnp.where(inside, F32(math.exp(-k * k / SPREAD)), F32(0))
    return total


def tap(offset):
    spread = offset.astype(F32)
    return jnp.where(jnp.abs(offset) <= RADIUS, jnp.exp(-(spread * spread) / SPREAD), 0.0)


def kernel(
    slc, az, rg, pairs_in, screen_out, motion_out,
    image, send, recv, acc, smap, rmap, plist, normal, inverse, design, weights,
    right, blocks, total, image_sem, send_sem, recv_sem, lend_sem, borrow_sem, part_send, part_recv,
):
    p = lax.axis_index("pairs")
    s = lax.axis_index("stripe")
    sz, sy, sx = s // 8, lax.rem(s // 4, 2), lax.rem(s, 4)

    loads = []
    for j in range(2):
        for c in range(2):
            load = pltpu.make_async_copy(
                slc.at[j, c],
                image.at[j, pl.ds(c * LINES, LINES), pl.ds(WIDTH, RANGE)],
                image_sem.at[2 * j + c],
            )
            load.start()
            loads.append(load)

    def peer(k):
        dz, dy, dx = offset_of(k)
        return lax.rem(sz + dz, 4) * 8 + lax.rem(sy + dy, 2) * 4 + lax.rem(sx + dx, 4)

    barrier = pltpu.get_barrier_semaphore()

    def greet(i, carry):
        pl.semaphore_signal(
            barrier, inc=1, device_id=(p, lax.rem(s + i, STRIPES)), device_id_type=MESH
        )
        return carry

    lax.fori_loop(1, STRIPES, greet, 0)
    for dp in range(1, GROUPS):
        for ds in (-1, 0, 1):
            pl.semaphore_signal(
                barrier,
                inc=1,
                device_id=(lax.rem(p + dp, GROUPS), lax.rem(s + ds + STRIPES, STRIPES)),
                device_id_type=MESH,
            )

    for j in range(2):
        date = p * BLOCK + s * 2 + j
        row = iota((LINES, LINES), 0)
        line = (row & ~31) + ((row & 7) << 2) + ((row >> 3) & 3)
        smap[j] = (iota((LINES, LINES), 1) == line + az[date]).astype(BF16)
        rmap[j] = (
            iota((3 * WIDTH, WIDTH), 0) == iota((3 * WIDTH, WIDTH), 1) + WIDTH + rg[date]
        ).astype(BF16)
        edge = jnp.zeros((2 * LINES, WIDTH), BF16)
        image[j, :, pl.ds(0, WIDTH)] = edge
        image[j, :, pl.ds(WIDTH + RANGE, WIDTH)] = edge
    for load in loads:
        load.wait()
    pl.semaphore_wait(barrier, STRIPES - 1 + 3 * (GROUPS - 1))

    def stripe_copy(c, k):
        target = peer(k)
        return pltpu.make_async_remote_copy(
            src_ref=send.at[c, target],
            dst_ref=recv.at[c, pl.ds(s * TILE, TILE)],
            send_sem=send_sem.at[c, k],
            recv_sem=recv_sem.at[c, k],
            device_id=(p, target),
            device_id_type=MESH,
        )

    def resample(k, carry):
        target = peer(k)
        start = pl.multiple_of(target * WIDTH, WIDTH)
        for j in range(2):
            moved = dot(image[j, :, pl.ds(start, 3 * WIDTH)], rmap[j]).astype(BF16)
            both = jnp.concatenate([moved[:LINES], moved[LINES:]], axis=1)
            shifted = dot(smap[j], both).astype(BF16)
            for c in range(GROUPS):
                for comp in range(2):
                    send[c, target, pl.ds(j * 64 + comp * CHUNK, CHUNK), :] = shifted[
                        c * CHUNK : (c + 1) * CHUNK, comp * WIDTH : (comp + 1) * WIDTH
                    ]

        @pl.when(k != SELF)
        def _():
            stripe_copy(0, k).start()

        return carry

    lax.fori_loop(0, STRIPES, resample, 0)

    for c in range(1, GROUPS):

        def launch(k, carry, c=c):
            @pl.when(k != SELF)
            def _():
                stripe_copy(c, k).start()

            return carry

        lax.fori_loop(0, STRIPES, launch, 0)

    for c in range(GROUPS):
        recv[c, pl.ds(s * TILE, TILE), :] = send[c, s]

    plist[...] = jnp.full((8, LIST), -100000, jnp.int32)
    plist[0:2, 0:1000] = pairs_in[...]
    refs, secs = plist[0:1, :], plist[1:2, :]
    ids = iota((DATES, LIST), 0)
    signed = ((ids == refs).astype(F32) - (ids == secs).astype(F32)).astype(BF16)
    eye = (iota((DATES, DATES), 0) == iota((DATES, DATES), 1)).astype(F32)
    normal[...] = dot_lanes(signed, signed) + F32(DAMPING) * eye
    inverse[...] = F32(START) * eye

    def newton(_, carry):
        held = inverse[...]
        inverse[...] = 2.0 * held - dot(held, dot(normal[...], held, HIGHEST), HIGHEST)
        return carry

    lax.fori_loop(0, NEWTON, newton, 0)

    local = refs - p * BLOCK
    inside = (local >= 0) & (local < BLOCK)
    code = jnp.where(inside, (secs - refs - 1) * BLOCK + local, -1)
    found = (iota((COMBOS, LIST), 0) == code).astype(F32).astype(BF16)
    present = dot_lanes(jnp.ones((8, LIST), BF16), found)[0:1, :]
    combo = iota((ROWS, COMBOS), 1)
    first = combo & (BLOCK - 1)
    second = first + (combo >> 6) + 1
    place = iota((ROWS, COMBOS), 0)
    plain = (place == first).astype(F32) - (place == second).astype(F32)
    design[...] = (plain * present).astype(BF16)

    held_in, held_out = iota((128, 128), 0), iota((128, 128), 1)
    same = (held_in >> 6) == (held_out >> 6)
    row_in, row_out = (held_in >> 3) & 7, (held_out >> 3) & 7
    col_in, col_out = held_in & 7, held_out & 7
    scale = edge_weight(row_out + p * MROWS, MROWS * GROUPS) * edge_weight(
        col_out + s * MROWS, MROWS * STRIPES
    )
    for ci in range(3):
        far = row_in + (p + ci - 1) * MROWS
        near = row_out + p * MROWS
        row_ok = same & (far >= 0) & (far < MROWS * GROUPS)
        row_tap = jnp.where(row_ok, tap(far - near), 0.0)
        for si in range(3):
            far = col_in + (s + si - 1) * MROWS
            near = col_out + s * MROWS
            col_ok = (far >= 0) & (far < MROWS * STRIPES)
            col_tap = jnp.where(col_ok, tap(far - near), 0.0)
            weights[3 * ci + si] = row_tap * col_tap / scale
    total[...] = jnp.zeros(total.shape, F32)

    def lend(c):
        return pltpu.make_async_remote_copy(
            src_ref=recv.at[c, pl.ds(0, AHEAD * TILE)],
            dst_ref=recv.at[c, pl.ds(STRIPES * TILE, AHEAD * TILE)],
            send_sem=lend_sem.at[c],
            recv_sem=borrow_sem.at[c],
            device_id=(lax.rem(p + GROUPS - 1, GROUPS), s),
            device_id_type=MESH,
        )

    def part(c, ci, ds):
        target = (c - ci + GROUPS) % GROUPS
        rel = lax.rem(p - target + GROUPS, GROUPS)
        slot = 3 * (ci + 1) + 1 - ds
        source = right.at[c]
        landing = blocks.at[slot, pl.ds(pl.multiple_of(rel * ROWS, 8), ROWS)]
        remote = pltpu.make_async_remote_copy(
            src_ref=source,
            dst_ref=landing,
            send_sem=part_send.at[c, slot],
            recv_sem=part_recv.at[rel, slot],
            device_id=(target, lax.rem(s + ds + STRIPES, STRIPES)),
            device_id_type=MESH,
        )
        return target, slot, rel, remote

    def chunk(c, carry):
        def arrive(k, inner):
            @pl.when(k != SELF)
            def _():
                arriving = stripe_copy(c, k)
                arriving.wait_send()
                arriving.wait_recv()

            return inner

        lax.fori_loop(0, STRIPES, arrive, 0)
        lend(c).start()

        def products(d, inner):
            base = pl.multiple_of(d * 64, 64)

            def held(offset):
                lines = recv[c, pl.ds(base + offset, CHUNK), :].astype(F32)
                return lines.reshape(4, MROWS, WIDTH)

            a, b = held(0), held(CHUNK)
            for gap in range(1, GAPS + 1):
                x, y = held(64 * gap), held(64 * gap + CHUNK)
                real = jnp.sum(a * x + b * y, axis=0)
                imag = jnp.sum(b * x - a * y, axis=0)
                row = pl.multiple_of(((gap - 1) * BLOCK + d) * 16, 16)
                acc[pl.ds(row, MROWS), :] = real
                acc[pl.ds(row + MROWS, MROWS), :] = imag
            return inner

        lax.fori_loop(0, BLOCK - GAPS, products, 0)
        lend(c).wait_recv()
        lax.fori_loop(BLOCK - GAPS, BLOCK, products, 0)

        looked = jnp.zeros((COMBOS, 128), F32)
        lane = iota((2 * WIDTH, 128), 0) & (WIDTH - 1)
        column = iota((2 * WIDTH, 128), 1)
        for q in range(16):
            summed = acc[pl.ds(q, COMBOS, stride=16), :]
            high = summed.astype(BF16)
            low = (summed - high.astype(F32)).astype(BF16)
            pool = jnp.where(column == q * MROWS + (lane >> 4), 1.0 / 64.0, 0.0).astype(BF16)
            looked = looked + dot(jnp.concatenate([high, low], axis=1), pool)
        right[c] = dot(design[...], looked.astype(BF16))
        return carry

    for c in range(GROUPS):
        chunk(c, 0)
        for ci in (-1, 0, 1):
            for ds in (-1, 0, 1):
                target, slot, rel, remote = part(c, ci, ds)
                if ds == 0:

                    @pl.when(target != p)
                    def _():
                        remote.start()

                    @pl.when(target == p)
                    def _():
                        blocks[slot, 0:ROWS, :] = right[c]
                else:
                    remote.start()
        lend(c).wait_send()

    for c in range(GROUPS):
        for ci in (-1, 0, 1):
            for ds in (-1, 0, 1):
                target, slot, rel, remote = part(c, ci, ds)
                if ds == 0:

                    @pl.when(target != p)
                    def _():
                        remote.wait_send()
                else:
                    remote.wait_send()
    for rel in range(GROUPS):
        for slot in range(9):
            if rel == 0 and slot % 3 == 1:
                continue
            pltpu.make_async_remote_copy(
                src_ref=right.at[0],
                dst_ref=blocks.at[slot, pl.ds(rel * ROWS, ROWS)],
                send_sem=part_send.at[0, slot],
                recv_sem=part_recv.at[rel, slot],
                device_id=(lax.rem(p + 1, GROUPS), s),
                device_id_type=MESH,
            ).wait_recv()

    smooth = dot(blocks[0], weights[0], HIGHEST)
    for slot in range(1, 9):
        smooth = smooth + dot(blocks[slot], weights[slot], HIGHEST)
    centre = blocks[4]
    for rel in range(GROUPS):
        group = lax.rem(p + rel, GROUPS)
        rows = pl.ds(pl.multiple_of(group * BLOCK, BLOCK), ROWS)
        cut = slice(rel * ROWS, (rel + 1) * ROWS)
        total[rows, 0:128] = total[rows, 0:128] + centre[cut]
        total[rows, 128:256] = total[rows, 128:256] + smooth[cut]
    solved = dot(inverse[...], total[0:DATES, :], HIGHEST)
    screen = solved[:, 128:256]
    screen_out[...] = screen.T
    motion_out[...] = (solved[:, 0:128] - screen).T


def local(slc_stack, az_offset, rg_offset, pair_list):
    vmem = pl.BlockSpec(memory_space=pltpu.VMEM)
    smem = pl.BlockSpec(memory_space=pltpu.SMEM)
    dma = pltpu.SemaphoreType.DMA
    result = jax.ShapeDtypeStruct((2 * MROWS * MROWS, DATES), F32)
    screen, motion = pl.pallas_call(
        kernel,
        out_shape=(result, result),
        in_specs=[pl.BlockSpec(memory_space=pl.ANY), smem, smem, vmem],
        out_specs=(vmem, vmem),
        scratch_shapes=[
            pltpu.VMEM((2, 2 * LINES, RANGE + 2 * WIDTH), BF16),
            pltpu.VMEM((GROUPS, STRIPES, TILE, WIDTH), BF16),
            pltpu.VMEM((GROUPS, (STRIPES + AHEAD) * TILE, WIDTH), BF16),
            pltpu.VMEM((COMBOS * 16, WIDTH), F32),
            pltpu.VMEM((2, LINES, LINES), BF16),
            pltpu.VMEM((2, 3 * WIDTH, WIDTH), BF16),
            pltpu.VMEM((8, LIST), jnp.int32),
            pltpu.VMEM((DATES, DATES), F32),
            pltpu.VMEM((DATES, DATES), F32),
            pltpu.VMEM((ROWS, COMBOS), BF16),
            pltpu.VMEM((9, 128, 128), F32),
            pltpu.VMEM((GROUPS, ROWS, 128), F32),
            pltpu.VMEM((9, GROUPS * ROWS, 128), F32),
            pltpu.VMEM(((GROUPS - 1) * BLOCK + ROWS, 256), F32),
            dma((4,)),
            dma((GROUPS, STRIPES)),
            dma((GROUPS, STRIPES)),
            dma((GROUPS,)),
            dma((GROUPS,)),
            dma((GROUPS, 9)),
            dma((GROUPS, 9)),
        ],
        compiler_params=pltpu.CompilerParams(
            collective_id=0, has_side_effects=True, vmem_limit_bytes=48 << 20
        ),
    )(slc_stack, az_offset, rg_offset, pair_list.T)

    def placed(value):
        return value.reshape(2, MROWS, MROWS, DATES).transpose(3, 0, 1, 2)

    return placed(screen), placed(motion)


def solution(mesh):
    return jax.shard_map(
        local,
        mesh=mesh,
        in_specs=(P(("pairs", "stripe"), None, None, None), P(), P(), P()),
        out_specs=(P(None, None, "pairs", "stripe"), P(None, None, "pairs", "stripe")),
        check_vma=False,
    )
```

```python
import math

import jax
import jax.numpy as jnp
from jax import lax
from jax.experimental import pallas as pl
from jax.experimental.pallas import tpu as pltpu
from jax.sharding import PartitionSpec as P

MESH = pl.DeviceIdType.MESH
HIGHEST = lax.Precision.HIGHEST
F32 = jnp.float32
BF16 = jnp.bfloat16

GROUPS = 4
STRIPES = 32
DATES = 256
BLOCK = 64
GAPS = 5
COMBOS = BLOCK * GAPS
LENT = GAPS * 64
LINES = 128
CHUNK = LINES // GROUPS
WIDTH = 128
RANGE = STRIPES * WIDTH
TILE = 128
MROWS = 8
ROWS = 72
LIST = 1024
RADIUS = 3
DAMPING = 0.5
NEWTON = 9
EAGER = 2
START = 2.0 / 21.0
SPREAD = 2.0 * (RADIUS / 2.0) ** 2


def iota(shape, dim):
    return lax.broadcasted_iota(jnp.int32, shape, dim)


def dot(a, b, precision=None):
    return lax.dot_general(
        a, b, (((1,), (0,)), ((), ())), precision=precision, preferred_element_type=F32
    )


def dot_lanes(a, b):
    return lax.dot_general(a, b, (((1,), (1,)), ((), ())), preferred_element_type=F32)


def offset_of(k):
    n = lax.rem(k + 1, 4)
    dx = n + n // 2 - 2 * (n // 3)
    dy = 1 - lax.rem(k, 8) // 4
    dz = lax.rem(dx + k // 8, 4)
    return dz, dy, dx


SELF = 7


def edge_weight(position, whole):
    total = jnp.zeros(position.shape, F32)
    for k in range(-RADIUS, RADIUS + 1):
        inside = (position + k >= 0) & (position + k < whole)
        total = total + jnp.where(inside, F32(math.exp(-k * k / SPREAD)), F32(0))
    return total


def tap(offset):
    spread = offset.astype(F32)
    return jnp.where(jnp.abs(offset) <= RADIUS, jnp.exp(-(spread * spread) / SPREAD), 0.0)


def kernel(
    slc, az_in, rg_in, pairs_in, screen_out, motion_out,
    az, rg, listed, image, send, recv, acc, smap, rmap, plist, normal, inverse, design, row_taps, col_taps, scale,
    right, blocks, total, small_sem, image_sem, send_sem, recv_sem, lend_sem, borrow_sem, part_send, part_recv,
):
    p = lax.axis_index("pairs")
    s = lax.axis_index("stripe")
    sz, sy, sx = s // 8, lax.rem(s // 4, 2), lax.rem(s, 4)

    small = []
    for n, (source, held) in enumerate(((az_in, az), (rg_in, rg), (pairs_in, listed))):
        small.append(pltpu.make_async_copy(source, held, small_sem.at[n]))
        small[n].start()
    loads = []
    for j in range(2):
        for c in range(2):
            load = pltpu.make_async_copy(
                slc.at[j, c],
                image.at[j, pl.ds(c * LINES, LINES), pl.ds(WIDTH, RANGE)],
                image_sem.at[2 * j + c],
            )
            load.start()
            loads.append(load)

    def peer(k):
        dz, dy, dx = offset_of(k)
        return lax.rem(sz + dz, 4) * 8 + lax.rem(sy + dy, 2) * 4 + lax.rem(sx + dx, 4)

    def turn_of(source):
        dz = lax.rem(sz - source // 8 + 4, 4)
        dy = lax.rem(sy - lax.rem(source // 4, 2) + 2, 2)
        dx = lax.rem(sx - lax.rem(source, 4) + 4, 4)
        n = dx + dx // 2 - 2 * (dx // 3)
        return lax.rem(dz - dx + 4, 4) * 8 + (1 - dy) * 4 + lax.rem(n + 3, 4)

    barrier = pltpu.get_barrier_semaphore()

    def greet(i, carry):
        pl.semaphore_signal(
            barrier, inc=1, device_id=(p, lax.rem(s + i, STRIPES)), device_id_type=MESH
        )
        return carry

    lax.fori_loop(1, STRIPES, greet, 0)
    for dp in range(1, GROUPS):
        for ds in (-1, 0, 1):
            pl.semaphore_signal(
                barrier,
                inc=1,
                device_id=(lax.rem(p + dp, GROUPS), lax.rem(s + ds + STRIPES, STRIPES)),
                device_id_type=MESH,
            )

    for load in small:
        load.wait()
    for j in range(2):
        date = p * BLOCK + s * 2 + j
        row = iota((LINES, LINES), 0)
        line = (row & ~31) + ((row & 7) << 2) + ((row >> 3) & 3)
        smap[j] = (iota((LINES, LINES), 1) == line + az[date]).astype(BF16)
        rmap[j] = (
            iota((3 * WIDTH, WIDTH), 0) == iota((3 * WIDTH, WIDTH), 1) + WIDTH + rg[date]
        ).astype(BF16)
        edge = jnp.zeros((2 * LINES, WIDTH), BF16)
        image[j, :, pl.ds(0, WIDTH)] = edge
        image[j, :, pl.ds(WIDTH + RANGE, WIDTH)] = edge
    for load in loads:
        load.wait()
    pl.semaphore_wait(barrier, STRIPES - 1 + 3 * (GROUPS - 1))

    def stripe_copy(c, k):
        target = peer(k)
        return pltpu.make_async_remote_copy(
            src_ref=send.at[c, target],
            dst_ref=recv.at[c, pl.ds(s * TILE, TILE)],
            send_sem=send_sem.at[c, k],
            recv_sem=recv_sem.at[c, k],
            device_id=(p, target),
            device_id_type=MESH,
        )

    def resample(k, carry):
        target = peer(k)
        start = pl.multiple_of(target * WIDTH, WIDTH)
        for j in range(2):
            moved = dot(image[j, :, pl.ds(start, 3 * WIDTH)], rmap[j]).astype(BF16)
            both = jnp.concatenate([moved[:LINES], moved[LINES:]], axis=1)
            shifted = dot(smap[j], both).astype(BF16)
            for c in range(GROUPS):
                for comp in range(2):
                    send[c, target, pl.ds(j * 64 + comp * CHUNK, CHUNK), :] = shifted[
                        c * CHUNK : (c + 1) * CHUNK, comp * WIDTH : (comp + 1) * WIDTH
                    ]

        @pl.when(k != SELF)
        def _():
            for c in range(EAGER):
                stripe_copy(c, k).start()

        return carry

    lax.fori_loop(0, STRIPES, resample, 0, unroll=2)

    for c in range(EAGER, GROUPS):

        def launch(k, carry, c=c):
            @pl.when(k != SELF)
            def _():
                stripe_copy(c, k).start()

            return carry

        lax.fori_loop(0, STRIPES, launch, 0)

    for c in range(GROUPS):
        recv[c, pl.ds(s * TILE, TILE), :] = send[c, s]

    plist[...] = jnp.full((8, LIST), -100000, jnp.int32)
    plist[0:2, 0:1000] = listed[...]
    refs, secs = plist[0:1, :], plist[1:2, :]
    ids = iota((DATES, LIST), 0)
    signed = ((ids == refs).astype(F32) - (ids == secs).astype(F32)).astype(BF16)
    eye = (iota((DATES, DATES), 0) == iota((DATES, DATES), 1)).astype(F32)
    normal[...] = dot_lanes(signed, signed) + F32(DAMPING) * eye
    inverse[...] = F32(START) * eye

    def newton(_, carry):
        held = inverse[...]
        inverse[...] = 2.0 * held - dot(held, dot(normal[...], held, HIGHEST), HIGHEST)
        return carry

    lax.fori_loop(0, NEWTON, newton, 0)

    local = refs - p * BLOCK
    inside = (local >= 0) & (local < BLOCK)
    code = jnp.where(inside, (secs - refs - 1) * BLOCK + local, -1)
    found = (iota((COMBOS, LIST), 0) == code).astype(F32).astype(BF16)
    present = dot_lanes(jnp.ones((8, LIST), BF16), found)[0:1, :]
    combo = iota((ROWS, COMBOS), 1)
    first = combo & (BLOCK - 1)
    second = first + (combo >> 6) + 1
    place = iota((ROWS, COMBOS), 0)
    plain = (place == first).astype(F32) - (place == second).astype(F32)
    design[...] = (plain * present).astype(BF16)

    held_in, held_out = iota((128, 128), 0), iota((128, 128), 1)
    same = (held_in >> 6) == (held_out >> 6)
    row_in, row_out = (held_in >> 3) & 7, (held_out >> 3) & 7
    col_in, col_out = held_in & 7, held_out & 7
    row_keep = same & (col_in == col_out)
    col_keep = same & (row_in == row_out)
    for n in range(3):
        shift = (n - 1) * MROWS
        row_taps[n] = jnp.where(row_keep, tap(row_in + shift - row_out), 0.0)
        far = col_in + s * MROWS + shift
        col_ok = col_keep & (far >= 0) & (far < MROWS * STRIPES)
        col_taps[n] = jnp.where(col_ok, tap(col_in + shift - col_out), 0.0)
    held_row = (iota((8, 128), 1) >> 3) & 7
    held_col = iota((8, 128), 1) & 7
    scale[...] = 1.0 / (
        edge_weight(held_row + p * MROWS, MROWS * GROUPS)
        * edge_weight(held_col + s * MROWS, MROWS * STRIPES)
    )
    total[...] = jnp.zeros(total.shape, F32)

    def lend(c):
        return pltpu.make_async_remote_copy(
            src_ref=recv.at[c, pl.ds(0, LENT)],
            dst_ref=recv.at[c, pl.ds(STRIPES * TILE, LENT)],
            send_sem=lend_sem.at[c],
            recv_sem=borrow_sem.at[c],
            device_id=(lax.rem(p + GROUPS - 1, GROUPS), s),
            device_id_type=MESH,
        )

    def part(target, slot):
        rel = lax.rem(p - target + GROUPS, GROUPS)
        ds = 0 if slot == 0 else 2 - slot
        return pltpu.make_async_remote_copy(
            src_ref=right.at[0 if slot == 0 else 1, target],
            dst_ref=blocks.at[slot, pl.ds(pl.multiple_of(rel * ROWS, 8), ROWS)],
            send_sem=part_send.at[target, slot],
            recv_sem=part_recv.at[rel, slot],
            device_id=(target, lax.rem(s + ds + STRIPES, STRIPES)),
            device_id_type=MESH,
        )

    def send_part(target, slot):
        if slot in (1, 3):
            part(target, slot).start()
            return

        @pl.when(p != target)
        def _():
            part(target, slot).start()

        @pl.when(p == target)
        def _():
            blocks[slot, 0:ROWS, :] = right[0 if slot == 0 else 1, target]

    def filter_rows(target):
        filtered = jnp.zeros((ROWS, 128), F32)
        for n in range(3):
            c = target + n - 1
            if 0 <= c < GROUPS:
                filtered = filtered + dot(right[0, c], row_taps[n], HIGHEST)
        right[1, target] = filtered
        for slot in (1, 3, 2):
            send_part(target, slot)

    def products_of(c):
        def products(d, inner):
            base = pl.multiple_of(d * 64, 64)

            def held(offset):
                lines = recv[c, pl.ds(base + offset, CHUNK), :].astype(F32)
                return lines.reshape(4, MROWS, WIDTH)

            a, b = held(0), held(CHUNK)
            for gap in range(1, GAPS + 1):
                x, y = held(64 * gap), held(64 * gap + CHUNK)
                real = jnp.sum(a * x + b * y, axis=0)
                imag = jnp.sum(b * x - a * y, axis=0)
                row = pl.multiple_of(((gap - 1) * BLOCK + d) * 16, 16)
                acc[c % 2, pl.ds(row, MROWS), :] = real
                acc[c % 2, pl.ds(row + MROWS, MROWS), :] = imag
            return inner

        return products

    def begin(c):
        def first(n, inner):
            @pl.when(s != n)
            def _():
                stripe_copy(c, turn_of(n)).wait_recv()

            return inner

        lax.fori_loop(0, 3, first, 0)
        lend(c).start()
        lax.fori_loop(3, STRIPES, first, 0)
        lax.fori_loop(0, BLOCK - GAPS, products_of(c), 0)

    def finish(c):
        lend(c).wait_recv()
        lax.fori_loop(BLOCK - GAPS, BLOCK, products_of(c), 0)
        looked = jnp.zeros((COMBOS, 128), F32)
        lane = iota((2 * WIDTH, 128), 0) & (WIDTH - 1)
        column = iota((2 * WIDTH, 128), 1)
        for q in range(16):
            summed = acc[c % 2, pl.ds(q, COMBOS, stride=16), :]
            high = summed.astype(BF16)
            low = (summed - high.astype(F32)).astype(BF16)
            pool = jnp.where(column == q * MROWS + (lane >> 4), 1.0 / 64.0, 0.0).astype(BF16)
            looked = looked + dot(jnp.concatenate([high, low], axis=1), pool)
        right[0, c] = dot(design[...], looked.astype(BF16))
        send_part(c, 0)
        if c > 0:
            filter_rows(c - 1)
        if c == GROUPS - 1:
            filter_rows(c)

    for c in range(GROUPS):
        begin(c)
        if c > 0:
            finish(c - 1)
    finish(GROUPS - 1)

    for c in range(GROUPS):
        lend(c).wait_send()

        def sent(k, carry, c=c):
            @pl.when(k != SELF)
            def _():
                stripe_copy(c, k).wait_send()

            return carry

        lax.fori_loop(0, STRIPES, sent, 0)

    for target in range(GROUPS):
        for slot in (1, 3):
            part(target, slot).wait_send()

        @pl.when(p != target)
        def _():
            for slot in (0, 2):
                part(target, slot).wait_send()

    for rel in range(GROUPS):
        for slot in range(4):
            if rel == 0 and slot in (0, 2):
                continue
            pltpu.make_async_remote_copy(
                src_ref=right.at[0, 0],
                dst_ref=blocks.at[slot, pl.ds(rel * ROWS, ROWS)],
                send_sem=part_send.at[0, slot],
                recv_sem=part_recv.at[rel, slot],
                device_id=(lax.rem(p + 1, GROUPS), s),
                device_id_type=MESH,
            ).wait_recv()

    smooth = dot(blocks[1], col_taps[0], HIGHEST)
    for n in range(1, 3):
        smooth = smooth + dot(blocks[n + 1], col_taps[n], HIGHEST)
    smooth = smooth * scale[0:1, :]
    centre = blocks[0]
    for rel in range(GROUPS):
        group = lax.rem(p + rel, GROUPS)
        rows = pl.ds(pl.multiple_of(group * BLOCK, BLOCK), ROWS)
        cut = slice(rel * ROWS, (rel + 1) * ROWS)
        total[rows, 0:128] = total[rows, 0:128] + centre[cut]
        total[rows, 128:256] = total[rows, 128:256] + smooth[cut]
    solved = dot(inverse[...], total[0:DATES, :], HIGHEST)
    screen = solved[:, 128:256]
    screen_out[...] = screen.T
    motion_out[...] = (solved[:, 0:128] - screen).T


def local(slc_stack, az_offset, rg_offset, pair_list):
    vmem = pl.BlockSpec(memory_space=pltpu.VMEM)
    dma = pltpu.SemaphoreType.DMA
    result = jax.ShapeDtypeStruct((2 * MROWS * MROWS, DATES), F32)
    screen, motion = pl.pallas_call(
        kernel,
        out_shape=(result, result),
        in_specs=[pl.BlockSpec(memory_space=pltpu.HBM)] * 4,
        out_specs=(vmem, vmem),
        scratch_shapes=[
            pltpu.SMEM((DATES,), jnp.int32),
            pltpu.SMEM((DATES,), jnp.int32),
            pltpu.VMEM((2, 1000), jnp.int32),
            pltpu.VMEM((2, 2 * LINES, RANGE + 2 * WIDTH), BF16),
            pltpu.VMEM((GROUPS, STRIPES, TILE, WIDTH), BF16),
            pltpu.VMEM((GROUPS, STRIPES * TILE + LENT, WIDTH), BF16),
            pltpu.VMEM((2, COMBOS * 16, WIDTH), F32),
            pltpu.VMEM((2, LINES, LINES), BF16),
            pltpu.VMEM((2, 3 * WIDTH, WIDTH), BF16),
            pltpu.VMEM((8, LIST), jnp.int32),
            pltpu.VMEM((DATES, DATES), F32),
            pltpu.VMEM((DATES, DATES), F32),
            pltpu.VMEM((ROWS, COMBOS), BF16),
            pltpu.VMEM((3, 128, 128), F32),
            pltpu.VMEM((3, 128, 128), F32),
            pltpu.VMEM((8, 128), F32),
            pltpu.VMEM((2, GROUPS, ROWS, 128), F32),
            pltpu.VMEM((4, GROUPS * ROWS, 128), F32),
            pltpu.VMEM(((GROUPS - 1) * BLOCK + ROWS, 256), F32),
            dma((3,)),
            dma((4,)),
            dma((GROUPS, STRIPES)),
            dma((GROUPS, STRIPES)),
            dma((GROUPS,)),
            dma((GROUPS,)),
            dma((GROUPS, 4)),
            dma((GROUPS, 4)),
        ],
        compiler_params=pltpu.CompilerParams(
            collective_id=0, has_side_effects=True, vmem_limit_bytes=(64 << 20) - (1 << 16)
        ),
    )(slc_stack, az_offset, rg_offset, pair_list.T)

    def placed(value):
        return value.reshape(2, MROWS, MROWS, DATES).transpose(3, 0, 1, 2)

    return placed(screen), placed(motion)


def solution(mesh):
    return jax.shard_map(
        local,
        mesh=mesh,
        in_specs=(P(("pairs", "stripe"), None, None, None), P(), P(), P()),
        out_specs=(P(None, None, "pairs", "stripe"), P(None, None, "pairs", "stripe")),
        check_vma=False,
    )
```

```python
import math

import jax
import jax.numpy as jnp
from jax import lax
from jax.experimental import pallas as pl
from jax.experimental.pallas import tpu as pltpu
from jax.sharding import PartitionSpec as P

MESH = pl.DeviceIdType.MESH
HIGHEST = lax.Precision.HIGHEST
F32 = jnp.float32
BF16 = jnp.bfloat16

GROUPS = 4
STRIPES = 32
DATES = 256
BLOCK = 64
GAPS = 5
COMBOS = BLOCK * GAPS
LENT = GAPS * 64
LINES = 128
CHUNK = LINES // GROUPS
WIDTH = 128
RANGE = STRIPES * WIDTH
TILE = 128
MROWS = 8
ROWS = 72
LIST = 1024
RADIUS = 3
DAMPING = 0.5
NEWTON = 9
EAGER = 2
START = 2.0 / 21.0
SPREAD = 2.0 * (RADIUS / 2.0) ** 2


def iota(shape, dim):
    return lax.broadcasted_iota(jnp.int32, shape, dim)


def dot(a, b, precision=None):
    return lax.dot_general(
        a, b, (((1,), (0,)), ((), ())), precision=precision, preferred_element_type=F32
    )


def split(value):
    high = value.astype(BF16)
    return high, (value - high.astype(F32)).astype(BF16)


def stacked(value):
    high, low = split(value)
    return jnp.concatenate([high, high, low], axis=0)


def dot_split(a, b):
    high, low = split(a)
    return dot(jnp.concatenate([high, low, high], axis=1), b)


def dot_lanes(a, b):
    return lax.dot_general(a, b, (((1,), (1,)), ((), ())), preferred_element_type=F32)


def offset_of(k):
    n = lax.rem(k + 1, 4)
    dx = n + n // 2 - 2 * (n // 3)
    dy = 1 - lax.rem(k, 8) // 4
    dz = lax.rem(dx + k // 8, 4)
    return dz, dy, dx


SELF = 7


def edge_weight(position, whole):
    total = jnp.zeros(position.shape, F32)
    for k in range(-RADIUS, RADIUS + 1):
        inside = (position + k >= 0) & (position + k < whole)
        total = total + jnp.where(inside, F32(math.exp(-k * k / SPREAD)), F32(0))
    return total


def tap(offset):
    spread = offset.astype(F32)
    return jnp.where(jnp.abs(offset) <= RADIUS, jnp.exp(-(spread * spread) / SPREAD), 0.0)


def kernel(
    slc, az_in, rg_in, pairs_in, solved_out,
    az, rg, listed, image, send, recv, acc, smap, rmap, plist, normal, inverse, design, row_taps, col_taps, scale, pool, solver,
    right, blocks, total, small_sem, image_sem, send_sem, recv_sem, lend_sem, borrow_sem, part_send, part_recv,
):
    p = lax.axis_index("pairs")
    s = lax.axis_index("stripe")
    sz, sy, sx = s // 8, lax.rem(s // 4, 2), lax.rem(s, 4)

    small = []
    for n, (source, held) in enumerate(((az_in, az), (rg_in, rg), (pairs_in, listed))):
        small.append(pltpu.make_async_copy(source, held, small_sem.at[n]))
        small[n].start()
    loads = []
    for j in range(2):
        for c in range(2):
            load = pltpu.make_async_copy(
                slc.at[j, c],
                image.at[j, pl.ds(c * LINES, LINES), pl.ds(WIDTH, RANGE)],
                image_sem.at[2 * j + c],
            )
            load.start()
            loads.append(load)

    def peer(k):
        dz, dy, dx = offset_of(k)
        return lax.rem(sz + dz, 4) * 8 + lax.rem(sy + dy, 2) * 4 + lax.rem(sx + dx, 4)

    def turn_of(source):
        dz = lax.rem(sz - source // 8 + 4, 4)
        dy = lax.rem(sy - lax.rem(source // 4, 2) + 2, 2)
        dx = lax.rem(sx - lax.rem(source, 4) + 4, 4)
        n = dx + dx // 2 - 2 * (dx // 3)
        return lax.rem(dz - dx + 4, 4) * 8 + (1 - dy) * 4 + lax.rem(n + 3, 4)

    barrier = pltpu.get_barrier_semaphore()

    def greet(i, carry):
        pl.semaphore_signal(
            barrier, inc=1, device_id=(p, lax.rem(s + i, STRIPES)), device_id_type=MESH
        )
        return carry

    lax.fori_loop(1, STRIPES, greet, 0)
    for dp in range(1, GROUPS):
        for ds in (-1, 0, 1):
            pl.semaphore_signal(
                barrier,
                inc=1,
                device_id=(lax.rem(p + dp, GROUPS), lax.rem(s + ds + STRIPES, STRIPES)),
                device_id_type=MESH,
            )

    for load in small:
        load.wait()
    for j in range(2):
        date = p * BLOCK + s * 2 + j
        row = iota((LINES, LINES), 0)
        line = (row & ~31) + ((row & 7) << 2) + ((row >> 3) & 3)
        smap[j] = (iota((LINES, LINES), 1) == line + az[date]).astype(BF16)
        rmap[j] = (
            iota((3 * WIDTH, WIDTH), 0) == iota((3 * WIDTH, WIDTH), 1) + WIDTH + rg[date]
        ).astype(BF16)
        edge = jnp.zeros((2 * LINES, WIDTH), BF16)
        image[j, :, pl.ds(0, WIDTH)] = edge
        image[j, :, pl.ds(WIDTH + RANGE, WIDTH)] = edge
    for load in loads:
        load.wait()
    pl.semaphore_wait(barrier, STRIPES - 1 + 3 * (GROUPS - 1))

    def stripe_copy(c, k):
        target = peer(k)
        return pltpu.make_async_remote_copy(
            src_ref=send.at[c, target],
            dst_ref=recv.at[c, pl.ds(s * TILE, TILE)],
            send_sem=send_sem.at[c, k],
            recv_sem=recv_sem.at[c, k],
            device_id=(p, target),
            device_id_type=MESH,
        )

    def resample(k, carry):
        target = peer(k)
        start = pl.multiple_of(target * WIDTH, WIDTH)
        for j in range(2):
            moved = dot(image[j, :, pl.ds(start, 3 * WIDTH)], rmap[j]).astype(BF16)
            both = jnp.concatenate([moved[:LINES], moved[LINES:]], axis=1)
            shifted = dot(smap[j], both).astype(BF16)
            for c in range(GROUPS):
                for comp in range(2):
                    send[c, target, pl.ds(j * 64 + comp * CHUNK, CHUNK), :] = shifted[
                        c * CHUNK : (c + 1) * CHUNK, comp * WIDTH : (comp + 1) * WIDTH
                    ]

        @pl.when(k != SELF)
        def _():
            for c in range(EAGER):
                stripe_copy(c, k).start()

        return carry

    lax.fori_loop(0, STRIPES, resample, 0, unroll=2)

    for c in range(EAGER, GROUPS):

        def launch(k, carry, c=c):
            @pl.when(k != SELF)
            def _():
                stripe_copy(c, k).start()

            return carry

        lax.fori_loop(0, STRIPES, launch, 0)

    for c in range(GROUPS):
        recv[c, pl.ds(s * TILE, TILE), :] = send[c, s]

    plist[...] = jnp.full((8, LIST), -100000, jnp.int32)
    plist[0:2, 0:1000] = listed[...]
    refs, secs = plist[0:1, :], plist[1:2, :]
    ids = iota((DATES, LIST), 0)
    signed = ((ids == refs).astype(F32) - (ids == secs).astype(F32)).astype(BF16)
    eye = (iota((DATES, DATES), 0) == iota((DATES, DATES), 1)).astype(F32)
    normal[...] = dot_lanes(signed, signed) + F32(DAMPING) * eye
    inverse[...] = F32(START) * eye

    def newton(_, carry):
        held = inverse[...]
        inverse[...] = 2.0 * held - dot(held, dot(normal[...], held, HIGHEST), HIGHEST)
        return carry

    lax.fori_loop(0, NEWTON, newton, 0)
    solver[...] = stacked(inverse[...])

    local = refs - p * BLOCK
    inside = (local >= 0) & (local < BLOCK)
    code = jnp.where(inside, (secs - refs - 1) * BLOCK + local, -1)
    found = (iota((COMBOS, LIST), 0) == code).astype(F32).astype(BF16)
    present = dot_lanes(jnp.ones((8, LIST), BF16), found)[0:1, :]
    combo = iota((ROWS, COMBOS), 1)
    first = combo & (BLOCK - 1)
    second = first + (combo >> 6) + 1
    place = iota((ROWS, COMBOS), 0)
    plain = (place == first).astype(F32) - (place == second).astype(F32)
    design[...] = (plain * present).astype(BF16)

    held_in, held_out = iota((128, 128), 0), iota((128, 128), 1)
    same = (held_in >> 6) == (held_out >> 6)
    row_in, row_out = (held_in >> 3) & 7, (held_out >> 3) & 7
    col_in, col_out = held_in & 7, held_out & 7
    row_keep = same & (col_in == col_out)
    col_keep = same & (row_in == row_out)
    for n in range(3):
        shift = (n - 1) * MROWS
        row_taps[n] = stacked(jnp.where(row_keep, tap(row_in + shift - row_out), 0.0))
        far = col_in + s * MROWS + shift
        col_ok = col_keep & (far >= 0) & (far < MROWS * STRIPES)
        col_taps[n] = stacked(jnp.where(col_ok, tap(col_in + shift - col_out), 0.0))
    held_row = (iota((8, 128), 1) >> 3) & 7
    held_col = iota((8, 128), 1) & 7
    scale[...] = 1.0 / (
        edge_weight(held_row + p * MROWS, MROWS * GROUPS)
        * edge_weight(held_col + s * MROWS, MROWS * STRIPES)
    )
    total[...] = jnp.zeros(total.shape, F32)
    lane = iota((2 * WIDTH, 128), 0) & (WIDTH - 1)
    column = iota((2 * WIDTH, 128), 1)
    for u in range(MROWS):
        hit = column == ((lane >> 3) & 1) * 64 + u * MROWS + (lane >> 4)
        pool[pl.ds(u * 2 * WIDTH, 2 * WIDTH), :] = jnp.where(hit, 1.0 / 64.0, 0.0).astype(BF16)

    def lend(c):
        return pltpu.make_async_remote_copy(
            src_ref=recv.at[c, pl.ds(0, LENT)],
            dst_ref=recv.at[c, pl.ds(STRIPES * TILE, LENT)],
            send_sem=lend_sem.at[c],
            recv_sem=borrow_sem.at[c],
            device_id=(lax.rem(p + GROUPS - 1, GROUPS), s),
            device_id_type=MESH,
        )

    def part(target, slot):
        rel = lax.rem(p - target + GROUPS, GROUPS)
        ds = 0 if slot == 0 else 2 - slot
        return pltpu.make_async_remote_copy(
            src_ref=right.at[0 if slot == 0 else 1, target],
            dst_ref=blocks.at[slot, pl.ds(pl.multiple_of(rel * ROWS, 8), ROWS)],
            send_sem=part_send.at[target, slot],
            recv_sem=part_recv.at[rel, slot],
            device_id=(target, lax.rem(s + ds + STRIPES, STRIPES)),
            device_id_type=MESH,
        )

    def send_part(target, slot):
        if slot in (1, 3):
            part(target, slot).start()
            return

        @pl.when(p != target)
        def _():
            part(target, slot).start()

        @pl.when(p == target)
        def _():
            blocks[slot, 0:ROWS, :] = right[0 if slot == 0 else 1, target]

    def filter_rows(target):
        filtered = jnp.zeros((ROWS, 128), F32)
        for n in range(3):
            c = target + n - 1
            if 0 <= c < GROUPS:
                filtered = filtered + dot_split(right[0, c], row_taps[n])
        right[1, target] = filtered
        for slot in (1, 3, 2):
            send_part(target, slot)

    def products_of(c):
        def products(d, inner):
            base = pl.multiple_of(d * 64, 64)

            def held(offset):
                lines = recv[c, pl.ds(base + offset, CHUNK), :].astype(F32)
                return lines.reshape(4, MROWS, WIDTH)

            a, b = held(0), held(CHUNK)
            for gap in range(1, GAPS + 1):
                x, y = held(64 * gap), held(64 * gap + CHUNK)
                real = jnp.sum(a * x + b * y, axis=0)
                imag = jnp.sum(b * x - a * y, axis=0)
                row = pl.multiple_of(((gap - 1) * BLOCK + d) * 16, 16)
                acc[c % 2, pl.ds(row, MROWS), :] = real
                acc[c % 2, pl.ds(row + MROWS, MROWS), :] = imag
            return inner

        return products

    def begin(c):
        def first(n, inner):
            @pl.when(s != n)
            def _():
                stripe_copy(c, turn_of(n)).wait_recv()

            return inner

        lax.fori_loop(0, 3, first, 0)
        lend(c).start()
        lax.fori_loop(3, STRIPES, first, 0)
        lax.fori_loop(0, BLOCK - GAPS - 1, products_of(c), 0, unroll=2)

    def finish(c):
        lend(c).wait_recv()
        lax.fori_loop(BLOCK - GAPS - 1, BLOCK, products_of(c), 0, unroll=2)
        front = (iota((COMBOS, WIDTH), 1) & 8) == 0
        cut = []
        for u in range(MROWS):
            real = acc[c % 2, pl.ds(u, COMBOS, stride=16), :]
            imag = acc[c % 2, pl.ds(u + MROWS, COMBOS, stride=16), :]
            real = real + pltpu.roll(real, WIDTH - 8, 1)
            imag = imag + pltpu.roll(imag, 8, 1)
            cut.extend(split(jnp.where(front, real, imag)))
        looked = dot(jnp.concatenate(cut, axis=1), pool[...])
        right[0, c] = dot(design[...], looked.astype(BF16))
        send_part(c, 0)
        if c > 0:
            filter_rows(c - 1)
        if c == GROUPS - 1:
            filter_rows(c)

    for c in range(GROUPS):
        begin(c)
        if c > 0:
            finish(c - 1)
    finish(GROUPS - 1)

    for c in range(GROUPS):
        lend(c).wait_send()

        def sent(k, carry, c=c):
            @pl.when(k != SELF)
            def _():
                stripe_copy(c, k).wait_send()

            return carry

        lax.fori_loop(0, STRIPES, sent, 0)

    for target in range(GROUPS):
        for slot in (1, 3):
            part(target, slot).wait_send()

        @pl.when(p != target)
        def _():
            for slot in (0, 2):
                part(target, slot).wait_send()

    for rel in range(GROUPS):
        for slot in range(4):
            if rel == 0 and slot in (0, 2):
                continue
            pltpu.make_async_remote_copy(
                src_ref=right.at[0, 0],
                dst_ref=blocks.at[slot, pl.ds(rel * ROWS, ROWS)],
                send_sem=part_send.at[0, slot],
                recv_sem=part_recv.at[rel, slot],
                device_id=(lax.rem(p + 1, GROUPS), s),
                device_id_type=MESH,
            ).wait_recv()

    smooth = dot_split(blocks[1], col_taps[0])
    for n in range(1, 3):
        smooth = smooth + dot_split(blocks[n + 1], col_taps[n])
    smooth = smooth * scale[0:1, :]
    centre = blocks[0]
    for rel in range(GROUPS):
        group = lax.rem(p + rel, GROUPS)
        rows = pl.ds(pl.multiple_of(group * BLOCK, BLOCK), ROWS)
        cut = slice(rel * ROWS, (rel + 1) * ROWS)
        total[rows, 0:128] = total[rows, 0:128] + centre[cut]
        total[rows, 128:256] = total[rows, 128:256] + smooth[cut]
    high, low = split(total[0:DATES, :])
    solved = dot(
        jnp.concatenate([high.T, low.T, high.T], axis=1), solver[...]
    )
    solved_out[...] = solved


def local(slc_stack, az_offset, rg_offset, pair_list):
    dma = pltpu.SemaphoreType.DMA
    solved = pl.pallas_call(
        kernel,
        out_shape=jax.ShapeDtypeStruct((2 * 2 * MROWS * MROWS, DATES), F32),
        in_specs=[pl.BlockSpec(memory_space=pltpu.HBM)] * 4,
        out_specs=pl.BlockSpec(memory_space=pltpu.VMEM),
        scratch_shapes=[
            pltpu.SMEM((DATES,), jnp.int32),
            pltpu.SMEM((DATES,), jnp.int32),
            pltpu.VMEM((2, 1000), jnp.int32),
            pltpu.VMEM((2, 2 * LINES, RANGE + 2 * WIDTH), BF16),
            pltpu.VMEM((GROUPS, STRIPES, TILE, WIDTH), BF16),
            pltpu.VMEM((GROUPS, STRIPES * TILE + LENT, WIDTH), BF16),
            pltpu.VMEM((2, COMBOS * 16, WIDTH), F32),
            pltpu.VMEM((2, LINES, LINES), BF16),
            pltpu.VMEM((2, 3 * WIDTH, WIDTH), BF16),
            pltpu.VMEM((8, LIST), jnp.int32),
            pltpu.VMEM((DATES, DATES), F32),
            pltpu.VMEM((DATES, DATES), F32),
            pltpu.VMEM((ROWS, COMBOS), BF16),
            pltpu.VMEM((3, 384, 128), BF16),
            pltpu.VMEM((3, 384, 128), BF16),
            pltpu.VMEM((8, 128), F32),
            pltpu.VMEM((MROWS * 2 * WIDTH, 128), BF16),
            pltpu.VMEM((3 * DATES, DATES), BF16),
            pltpu.VMEM((2, GROUPS, ROWS, 128), F32),
            pltpu.VMEM((4, GROUPS * ROWS, 128), F32),
            pltpu.VMEM(((GROUPS - 1) * BLOCK + ROWS, 256), F32),
            dma((3,)),
            dma((4,)),
            dma((GROUPS, STRIPES)),
            dma((GROUPS, STRIPES)),
            dma((GROUPS,)),
            dma((GROUPS,)),
            dma((GROUPS, 4)),
            dma((GROUPS, 4)),
        ],
        compiler_params=pltpu.CompilerParams(
            collective_id=0, has_side_effects=True, vmem_limit_bytes=(64 << 20) - (1 << 16)
        ),
    )(slc_stack, az_offset, rg_offset, pair_list.T)

    def placed(value):
        return value.reshape(2, MROWS, MROWS, DATES).transpose(3, 0, 1, 2)

    series, screen = solved[:128], solved[128:]
    return placed(screen), placed(series - screen)


def solution(mesh):
    return jax.shard_map(
        local,
        mesh=mesh,
        in_specs=(P(("pairs", "stripe"), None, None, None), P(), P(), P()),
        out_specs=(P(None, None, "pairs", "stripe"), P(None, None, "pairs", "stripe")),
        check_vma=False,
    )
```

```python
import math

import jax
import jax.numpy as jnp
from jax import lax
from jax.experimental import pallas as pl
from jax.experimental.pallas import tpu as pltpu
from jax.sharding import PartitionSpec as P

MESH = pl.DeviceIdType.MESH
HIGHEST = lax.Precision.HIGHEST
F32 = jnp.float32
BF16 = jnp.bfloat16

GROUPS = 4
STRIPES = 32
DATES = 256
BLOCK = 64
GAPS = 5
COMBOS = BLOCK * GAPS
LENT = GAPS * 64
LINES = 128
CHUNK = LINES // GROUPS
WIDTH = 128
RANGE = STRIPES * WIDTH
TILE = 128
MROWS = 8
ROWS = 72
LIST = 1024
RADIUS = 3
DAMPING = 0.5
NEWTON = 9
EAGER = 2
START = 2.0 / 21.0
SPREAD = 2.0 * (RADIUS / 2.0) ** 2


def iota(shape, dim):
    return lax.broadcasted_iota(jnp.int32, shape, dim)


def dot(a, b, precision=None):
    return lax.dot_general(
        a, b, (((1,), (0,)), ((), ())), precision=precision, preferred_element_type=F32
    )


def split(value):
    high = value.astype(BF16)
    return high, (value - high.astype(F32)).astype(BF16)


def stacked(value):
    high, low = split(value)
    return jnp.concatenate([high, high, low], axis=0)


def dot_split(a, b):
    high, low = split(a)
    return dot(jnp.concatenate([high, low, high], axis=1), b)


def dot_lanes(a, b):
    return lax.dot_general(a, b, (((1,), (1,)), ((), ())), preferred_element_type=F32)


def offset_of(k):
    n = lax.rem(k + 1, 4)
    dx = n + n // 2 - 2 * (n // 3)
    dy = 1 - lax.rem(k, 8) // 4
    dz = lax.rem(dx + k // 8, 4)
    return dz, dy, dx


SELF = 7


def edge_weight(position, whole):
    total = jnp.zeros(position.shape, F32)
    for k in range(-RADIUS, RADIUS + 1):
        inside = (position + k >= 0) & (position + k < whole)
        total = total + jnp.where(inside, F32(math.exp(-k * k / SPREAD)), F32(0))
    return total


def tap(offset):
    spread = offset.astype(F32)
    return jnp.where(jnp.abs(offset) <= RADIUS, jnp.exp(-(spread * spread) / SPREAD), 0.0)


def kernel(
    slc, az_in, rg_in, pairs_in, solved_out,
    az, rg, listed, image, send, recv, acc, smap, rmap, plist, normal, inverse, design, row_taps, col_taps, scale, pool, solver,
    right, blocks, total, small_sem, image_sem, send_sem, recv_sem, lend_sem, borrow_sem, part_send, part_recv,
):
    p = lax.axis_index("pairs")
    s = lax.axis_index("stripe")
    sz, sy, sx = s // 8, lax.rem(s // 4, 2), lax.rem(s, 4)

    small = []
    for n, (source, held) in enumerate(((az_in, az), (rg_in, rg), (pairs_in, listed))):
        small.append(pltpu.make_async_copy(source, held, small_sem.at[n]))
        small[n].start()
    loads = []
    for j in range(2):
        for c in range(2):
            load = pltpu.make_async_copy(
                slc.at[j, c],
                image.at[j, pl.ds(c * LINES, LINES), pl.ds(WIDTH, RANGE)],
                image_sem.at[2 * j + c],
            )
            load.start()
            loads.append(load)

    def peer(k):
        dz, dy, dx = offset_of(k)
        return lax.rem(sz + dz, 4) * 8 + lax.rem(sy + dy, 2) * 4 + lax.rem(sx + dx, 4)

    def turn_of(source):
        dz = lax.rem(sz - source // 8 + 4, 4)
        dy = lax.rem(sy - lax.rem(source // 4, 2) + 2, 2)
        dx = lax.rem(sx - lax.rem(source, 4) + 4, 4)
        n = dx + dx // 2 - 2 * (dx // 3)
        return lax.rem(dz - dx + 4, 4) * 8 + (1 - dy) * 4 + lax.rem(n + 3, 4)

    barrier = pltpu.get_barrier_semaphore()

    def greet(i, carry):
        pl.semaphore_signal(
            barrier, inc=1, device_id=(p, lax.rem(s + i, STRIPES)), device_id_type=MESH
        )
        return carry

    lax.fori_loop(1, STRIPES, greet, 0)
    for dp in range(1, GROUPS):
        for ds in (-1, 0, 1):
            pl.semaphore_signal(
                barrier,
                inc=1,
                device_id=(lax.rem(p + dp, GROUPS), lax.rem(s + ds + STRIPES, STRIPES)),
                device_id_type=MESH,
            )

    for load in small:
        load.wait()
    for j in range(2):
        date = p * BLOCK + s * 2 + j
        row = iota((LINES, LINES), 0)
        line = (row & ~31) + ((row & 7) << 2) + ((row >> 3) & 3)
        smap[j] = (iota((LINES, LINES), 1) == line + az[date]).astype(BF16)
        rmap[j] = (
            iota((3 * WIDTH, WIDTH), 0) == iota((3 * WIDTH, WIDTH), 1) + WIDTH + rg[date]
        ).astype(BF16)
        edge = jnp.zeros((2 * LINES, WIDTH), BF16)
        image[j, :, pl.ds(0, WIDTH)] = edge
        image[j, :, pl.ds(WIDTH + RANGE, WIDTH)] = edge
    for load in loads:
        load.wait()
    pl.semaphore_wait(barrier, STRIPES - 1 + 3 * (GROUPS - 1))

    def stripe_copy(c, k):
        target = peer(k)
        return pltpu.make_async_remote_copy(
            src_ref=send.at[c, target],
            dst_ref=recv.at[c, pl.ds(s * TILE, TILE)],
            send_sem=send_sem.at[c],
            recv_sem=recv_sem.at[c],
            device_id=(p, target),
            device_id_type=MESH,
        )

    def resample(k, carry):
        target = peer(k)
        start = pl.multiple_of(target * WIDTH, WIDTH)
        for j in range(2):
            moved = dot(image[j, :, pl.ds(start, 3 * WIDTH)], rmap[j]).astype(BF16)
            both = jnp.concatenate([moved[:LINES], moved[LINES:]], axis=1)
            shifted = dot(smap[j], both).astype(BF16)
            for c in range(GROUPS):
                for comp in range(2):
                    send[c, target, pl.ds(j * 64 + comp * CHUNK, CHUNK), :] = shifted[
                        c * CHUNK : (c + 1) * CHUNK, comp * WIDTH : (comp + 1) * WIDTH
                    ]

        @pl.when(k != SELF)
        def _():
            for c in range(EAGER):
                stripe_copy(c, k).start()

        return carry

    lax.fori_loop(0, STRIPES, resample, 0, unroll=2)

    for c in range(EAGER, GROUPS):

        def launch(k, carry, c=c):
            @pl.when(k != SELF)
            def _():
                stripe_copy(c, k).start()

            return carry

        lax.fori_loop(0, STRIPES, launch, 0)

    for c in range(GROUPS):
        recv[c, pl.ds(s * TILE, TILE), :] = send[c, s]

    plist[...] = jnp.full((8, LIST), -100000, jnp.int32)
    plist[0:2, 0:1000] = listed[...]
    refs, secs = plist[0:1, :], plist[1:2, :]
    ids = iota((DATES, LIST), 0)
    signed = ((ids == refs).astype(F32) - (ids == secs).astype(F32)).astype(BF16)
    eye = (iota((DATES, DATES), 0) == iota((DATES, DATES), 1)).astype(F32)
    normal[...] = dot_lanes(signed, signed) + F32(DAMPING) * eye
    inverse[...] = F32(START) * eye

    def newton(_, carry):
        held = inverse[...]
        inverse[...] = 2.0 * held - dot(held, dot(normal[...], held, HIGHEST), HIGHEST)
        return carry

    lax.fori_loop(0, NEWTON, newton, 0)
    solver[...] = stacked(inverse[...])

    local = refs - p * BLOCK
    inside = (local >= 0) & (local < BLOCK)
    code = jnp.where(inside, (secs - refs - 1) * BLOCK + local, -1)
    found = (iota((COMBOS, LIST), 0) == code).astype(F32).astype(BF16)
    present = dot_lanes(jnp.ones((8, LIST), BF16), found)[0:1, :]
    combo = iota((ROWS, COMBOS), 1)
    first = combo & (BLOCK - 1)
    second = first + (combo >> 6) + 1
    place = iota((ROWS, COMBOS), 0)
    plain = (place == first).astype(F32) - (place == second).astype(F32)
    design[...] = (plain * present).astype(BF16)

    held_in, held_out = iota((128, 128), 0), iota((128, 128), 1)
    same = (held_in >> 6) == (held_out >> 6)
    row_in, row_out = (held_in >> 3) & 7, (held_out >> 3) & 7
    col_in, col_out = held_in & 7, held_out & 7
    row_keep = same & (col_in == col_out)
    col_keep = same & (row_in == row_out)
    for n in range(3):
        shift = (n - 1) * MROWS
        row_taps[n] = stacked(jnp.where(row_keep, tap(row_in + shift - row_out), 0.0))
        far = col_in + s * MROWS + shift
        col_ok = col_keep & (far >= 0) & (far < MROWS * STRIPES)
        col_taps[n] = stacked(jnp.where(col_ok, tap(col_in + shift - col_out), 0.0))
    held_row = (iota((8, 128), 1) >> 3) & 7
    held_col = iota((8, 128), 1) & 7
    scale[...] = 1.0 / (
        edge_weight(held_row + p * MROWS, MROWS * GROUPS)
        * edge_weight(held_col + s * MROWS, MROWS * STRIPES)
    )
    total[...] = jnp.zeros(total.shape, F32)
    lane = iota((2 * WIDTH, 128), 0) & (WIDTH - 1)
    column = iota((2 * WIDTH, 128), 1)
    for u in range(MROWS):
        hit = column == ((lane >> 3) & 1) * 64 + u * MROWS + (lane >> 4)
        pool[pl.ds(u * 2 * WIDTH, 2 * WIDTH), :] = jnp.where(hit, 1.0 / 64.0, 0.0).astype(BF16)

    def lend(c):
        return pltpu.make_async_remote_copy(
            src_ref=recv.at[c, pl.ds(0, LENT)],
            dst_ref=recv.at[c, pl.ds(STRIPES * TILE, LENT)],
            send_sem=lend_sem.at[c],
            recv_sem=borrow_sem.at[c],
            device_id=(lax.rem(p + GROUPS - 1, GROUPS), s),
            device_id_type=MESH,
        )

    def part(target, slot):
        rel = lax.rem(p - target + GROUPS, GROUPS)
        ds = 0 if slot == 0 else 2 - slot
        return pltpu.make_async_remote_copy(
            src_ref=right.at[0 if slot == 0 else 1, target],
            dst_ref=blocks.at[slot, pl.ds(pl.multiple_of(rel * ROWS, 8), ROWS)],
            send_sem=part_send.at[target, slot],
            recv_sem=part_recv.at[rel, slot],
            device_id=(target, lax.rem(s + ds + STRIPES, STRIPES)),
            device_id_type=MESH,
        )

    def send_part(target, slot):
        if slot in (1, 3):
            part(target, slot).start()
            return

        @pl.when(p != target)
        def _():
            part(target, slot).start()

        @pl.when(p == target)
        def _():
            blocks[slot, 0:ROWS, :] = right[0 if slot == 0 else 1, target]

    def filter_rows(target):
        filtered = jnp.zeros((ROWS, 128), F32)
        for n in range(3):
            c = target + n - 1
            if 0 <= c < GROUPS:
                filtered = filtered + dot_split(right[0, c], row_taps[n])
        right[1, target] = filtered
        for slot in (1, 3, 2):
            send_part(target, slot)

    def products_of(c):
        def products(d, inner):
            base = pl.multiple_of(d * 64, 64)

            def held(offset):
                lines = recv[c, pl.ds(base + offset, CHUNK), :].astype(F32)
                return lines.reshape(4, MROWS, WIDTH)

            a, b = held(0), held(CHUNK)
            for gap in range(1, GAPS + 1):
                x, y = held(64 * gap), held(64 * gap + CHUNK)
                real = jnp.sum(a * x + b * y, axis=0)
                imag = jnp.sum(b * x - a * y, axis=0)
                row = pl.multiple_of(((gap - 1) * BLOCK + d) * 16, 16)
                acc[c % 2, pl.ds(row, MROWS), :] = real
                acc[c % 2, pl.ds(row + MROWS, MROWS), :] = imag
            return inner

        return products

    def begin(c):
        arrived = send.at[c, pl.ds(0, STRIPES - 1)]
        pltpu.make_async_remote_copy(
            src_ref=arrived,
            dst_ref=arrived,
            send_sem=send_sem.at[c],
            recv_sem=recv_sem.at[c],
            device_id=(p, peer(0)),
            device_id_type=MESH,
        ).wait_recv()
        lend(c).start()
        lax.fori_loop(0, BLOCK - GAPS - 1, products_of(c), 0, unroll=2)

    def finish(c):
        lend(c).wait_recv()
        lax.fori_loop(BLOCK - GAPS - 1, BLOCK, products_of(c), 0, unroll=2)
        front = (iota((COMBOS, WIDTH), 1) & 8) == 0
        cut = []
        for u in range(MROWS):
            real = acc[c % 2, pl.ds(u, COMBOS, stride=16), :]
            imag = acc[c % 2, pl.ds(u + MROWS, COMBOS, stride=16), :]
            real = real + pltpu.roll(real, WIDTH - 8, 1)
            imag = imag + pltpu.roll(imag, 8, 1)
            cut.extend(split(jnp.where(front, real, imag)))
        looked = dot(jnp.concatenate(cut, axis=1), pool[...])
        right[0, c] = dot(design[...], looked.astype(BF16))
        send_part(c, 0)
        if c > 0:
            filter_rows(c - 1)
        if c == GROUPS - 1:
            filter_rows(c)

    for c in range(GROUPS):
        begin(c)
        if c > 0:
            finish(c - 1)
    finish(GROUPS - 1)

    for c in range(GROUPS):
        lend(c).wait_send()

        all_sent = send.at[c, pl.ds(0, STRIPES - 1)]
        pltpu.make_async_remote_copy(
            src_ref=all_sent,
            dst_ref=all_sent,
            send_sem=send_sem.at[c],
            recv_sem=recv_sem.at[c],
            device_id=(p, peer(0)),
            device_id_type=MESH,
        ).wait_send()

    for target in range(GROUPS):
        for slot in (1, 3):
            part(target, slot).wait_send()

        @pl.when(p != target)
        def _():
            for slot in (0, 2):
                part(target, slot).wait_send()

    for rel in range(GROUPS):
        for slot in range(4):
            if rel == 0 and slot in (0, 2):
                continue
            pltpu.make_async_remote_copy(
                src_ref=right.at[0, 0],
                dst_ref=blocks.at[slot, pl.ds(rel * ROWS, ROWS)],
                send_sem=part_send.at[0, slot],
                recv_sem=part_recv.at[rel, slot],
                device_id=(lax.rem(p + 1, GROUPS), s),
                device_id_type=MESH,
            ).wait_recv()

    smooth = dot_split(blocks[1], col_taps[0])
    for n in range(1, 3):
        smooth = smooth + dot_split(blocks[n + 1], col_taps[n])
    smooth = smooth * scale[0:1, :]
    centre = blocks[0]
    for rel in range(GROUPS):
        group = lax.rem(p + rel, GROUPS)
        rows = pl.ds(pl.multiple_of(group * BLOCK, BLOCK), ROWS)
        cut = slice(rel * ROWS, (rel + 1) * ROWS)
        total[rows, 0:128] = total[rows, 0:128] + centre[cut]
        total[rows, 128:256] = total[rows, 128:256] + smooth[cut]
    high, low = split(total[0:DATES, :])
    solved = dot(
        jnp.concatenate([high.T, low.T, high.T], axis=1), solver[...]
    )
    solved_out[...] = solved


def local(slc_stack, az_offset, rg_offset, pair_list):
    dma = pltpu.SemaphoreType.DMA
    solved = pl.pallas_call(
        kernel,
        out_shape=jax.ShapeDtypeStruct((2 * 2 * MROWS * MROWS, DATES), F32),
        in_specs=[pl.BlockSpec(memory_space=pltpu.HBM)] * 4,
        out_specs=pl.BlockSpec(memory_space=pltpu.VMEM),
        scratch_shapes=[
            pltpu.SMEM((DATES,), jnp.int32),
            pltpu.SMEM((DATES,), jnp.int32),
            pltpu.VMEM((2, 1000), jnp.int32),
            pltpu.VMEM((2, 2 * LINES, RANGE + 2 * WIDTH), BF16),
            pltpu.VMEM((GROUPS, STRIPES, TILE, WIDTH), BF16),
            pltpu.VMEM((GROUPS, STRIPES * TILE + LENT, WIDTH), BF16),
            pltpu.VMEM((2, COMBOS * 16, WIDTH), F32),
            pltpu.VMEM((2, LINES, LINES), BF16),
            pltpu.VMEM((2, 3 * WIDTH, WIDTH), BF16),
            pltpu.VMEM((8, LIST), jnp.int32),
            pltpu.VMEM((DATES, DATES), F32),
            pltpu.VMEM((DATES, DATES), F32),
            pltpu.VMEM((ROWS, COMBOS), BF16),
            pltpu.VMEM((3, 384, 128), BF16),
            pltpu.VMEM((3, 384, 128), BF16),
            pltpu.VMEM((8, 128), F32),
            pltpu.VMEM((MROWS * 2 * WIDTH, 128), BF16),
            pltpu.VMEM((3 * DATES, DATES), BF16),
            pltpu.VMEM((2, GROUPS, ROWS, 128), F32),
            pltpu.VMEM((4, GROUPS * ROWS, 128), F32),
            pltpu.VMEM(((GROUPS - 1) * BLOCK + ROWS, 256), F32),
            dma((3,)),
            dma((4,)),
            dma((GROUPS,)),
            dma((GROUPS,)),
            dma((GROUPS,)),
            dma((GROUPS,)),
            dma((GROUPS, 4)),
            dma((GROUPS, 4)),
        ],
        compiler_params=pltpu.CompilerParams(
            collective_id=0, has_side_effects=True, vmem_limit_bytes=(64 << 20) - (1 << 16)
        ),
    )(slc_stack, az_offset, rg_offset, pair_list.T)

    def placed(value):
        return value.reshape(2, MROWS, MROWS, DATES).transpose(3, 0, 1, 2)

    series, screen = solved[:128], solved[128:]
    return placed(screen), placed(series - screen)


def solution(mesh):
    return jax.shard_map(
        local,
        mesh=mesh,
        in_specs=(P(("pairs", "stripe"), None, None, None), P(), P(), P()),
        out_specs=(P(None, None, "pairs", "stripe"), P(None, None, "pairs", "stripe")),
        check_vma=False,
    )
```
